32 devices in a mesh: clip: 8 (over y, x, core), cap: 4 (over z).
Axes of the slice: x: 2, y: 2, z: 4, core: 2. Of those that a mesh axis runs over, the one named last changes fastest.
Arguments:
- teacher_audio: bfloat16 [6144, 512], P(('clip', 'cap')), may hold values from -2 to 2
- teacher_text: bfloat16 [6144, 512], P(('cap', 'clip')), may hold values from -2 to 2
- student_audio: bfloat16 [6144, 512], P(('clip', 'cap')), may hold values from -2 to 2
- student_text: bfloat16 [6144, 512], P(('cap', 'clip')), may hold values from -2 to 2
Outputs:
- audio_grad: float32 [6144, 512], P(('clip', 'cap'))
- text_grad: float32 [6144, 512], P(('cap', 'clip'))
The draws below stay inside these ranges and needn't reach their ends.
All inputs are finite; a program needn't handle non-finite values.
Results may differ from the reference program's by a relative error of at most 0.0026.
Values may be sent and summed in bfloat16 or wider, within the bound.
A program may use at most 128 MiB of HBM per device.

```python
import math
import jax
import jax.numpy as jnp
from jax import lax

D = 512
ITERS = 3
PAIRS = 6144


def embed_pair(key):
    key_audio = jax.random.fold_in(key, 0)
    key_text = jax.random.fold_in(key, 1)
    key_scale_a = jax.random.fold_in(key, 3)
    key_scale_t = jax.random.fold_in(key, 4)
    spread_base = 0.55 * D ** (-0.25)
    scale_range = 0.55
    audio_rows = spread_base * jnp.clip(jax.random.normal(key_audio, (PAIRS, D), jnp.float32), -4.0, 4.0)
    audio_rows = audio_rows * jnp.exp(jax.random.uniform(key_scale_a, (PAIRS, 1), jnp.float32, -scale_range, scale_range))
    text_rows = spread_base * jnp.clip(jax.random.normal(key_text, (PAIRS, D), jnp.float32), -4.0, 4.0)
    text_rows = text_rows * jnp.exp(jax.random.uniform(key_scale_t, (PAIRS, 1), jnp.float32, -scale_range, scale_range))
    return (audio_rows, text_rows)


def draw_teacher_audio(key, part):
    return embed_pair(jax.random.fold_in(key, 11))[0].astype(jnp.bfloat16)


def draw_teacher_text(key, part):
    return embed_pair(jax.random.fold_in(key, 11))[1].astype(jnp.bfloat16)


def draw_student_audio(key, part):
    return embed_pair(jax.random.fold_in(key, 23))[0].astype(jnp.bfloat16)


def draw_student_text(key, part):
    return embed_pair(jax.random.fold_in(key, 23))[1].astype(jnp.bfloat16)


def setup_inputs(seed: int = 0) -> dict:
    keys = jax.random.split(jax.random.key(seed), 5)
    return {
        "teacher_audio": draw_teacher_audio(jax.random.fold_in(keys[4], 71), 0),
        "teacher_text": draw_teacher_text(jax.random.fold_in(keys[4], 71), 0),
        "student_audio": draw_student_audio(jax.random.fold_in(keys[4], 71), 0),
        "student_text": draw_student_text(jax.random.fold_in(keys[4], 71), 0),
    }


def teacher_kernel(row_block, teacher_text):
    logits = 10.0 * jnp.dot(row_block, teacher_text.T, preferred_element_type=jnp.float32)
    return jnp.exp(logits - jnp.max(logits, axis=1, keepdims=True))


def reference(teacher_audio, teacher_text, student_audio, student_text):
    block_size = math.gcd(PAIRS, 1024)
    block_count = PAIRS // block_size
    audio_blocks = teacher_audio.reshape(block_count, block_size, D)
    student_blocks = student_audio.reshape(block_count, block_size, D)

    def first_pass(running, row_block):
        kernel = teacher_kernel(row_block, teacher_text)
        return running + jnp.sum(kernel, axis=0), None

    column, _ = lax.scan(first_pass, jnp.zeros((PAIRS,), jnp.float32), audio_blocks)
    column_scale = 1.0 / column
    weights_row = None
    for sweep_index in range(ITERS):
        column_scale = 1.0 / column

        def sweep(running, row_block, scale_now=column_scale):
            kernel = teacher_kernel(row_block, teacher_text)
            weights = 1.0 / jnp.dot(kernel, scale_now, precision=lax.Precision.HIGHEST)
            return running + jnp.dot(weights, kernel, precision=lax.Precision.HIGHEST), weights

        column, weights_row = lax.scan(sweep, jnp.zeros((PAIRS,), jnp.float32), audio_blocks)

    def final_pass(running, inputs):
        row_block, weight_block, student_block = inputs
        kernel = teacher_kernel(row_block, teacher_text)
        target = (weight_block[:, None] * kernel) * column_scale[None, :]
        logits = 10.0 * jnp.dot(student_block, student_text.T, preferred_element_type=jnp.float32)
        student_exp = jnp.exp(logits - jnp.max(logits, axis=1, keepdims=True))
        student_prob = student_exp / jnp.sum(student_exp, axis=1, keepdims=True)
        residual = (student_prob - target).astype(jnp.bfloat16)
        audio_part = 10.0 * jnp.dot(residual, student_text, preferred_element_type=jnp.float32)
        text_part = 10.0 * jnp.dot(residual.T, student_block, preferred_element_type=jnp.float32)
        return running + text_part, audio_part

    text_grad, audio_parts = lax.scan(final_pass, jnp.zeros((PAIRS, D), jnp.float32),
                                      (audio_blocks, weights_row, student_blocks))
    return audio_parts.reshape(PAIRS, D), text_grad
```

```python
import functools

import jax
import jax.numpy as jnp
from jax import lax
from jax.experimental import pallas as pl
from jax.experimental.pallas import tpu as pltpu
from jax.sharding import PartitionSpec as P

ITERS = 3
LANE = 128
MESH = pl.DeviceIdType.MESH


def flip(index, bit):
    return index + bit * (1 - 2 * ((index // bit) % 2))


def flip_mask(index, mask, count):
    bit = 1
    while bit < count:
        if mask & bit:
            index = flip(index, bit)
        bit *= 2
    return index


def tree_orders(count):
    bits = []
    bit = 2
    while bit < count:
        bits.append(bit)
        bit *= 2
    tail = [1] if count > 1 else []
    return (bits + tail, bits[::-1] + tail)


def children(mask, order):
    last = -1
    for position, bit in enumerate(order):
        if mask & bit:
            last = position
    return [bit for bit in order[last + 1:]]


def mask_sequence(count, order):
    out, level = [], [0]
    while level:
        following = []
        for mask in level:
            for bit in children(mask, order):
                following.append(mask | bit)
        out.extend(following)
        level = following
    return out


def kernel(
    nclip, ncap, shard,
    ta_ref, tt_ref, sa_ref, st_ref, ag_ref, tg_ref,
    abuf, tbuf, kmat, smat, rmat, lbuf, pbuf, wrep, srep, crep, mrep, smax, ssum,
    rowx, colx, maxx, lastx, asend, arecv, tsend, trecv,
    az_send, az_recv, tx_send, tx_recv, rx_send, rx_recv, cx_send, cx_recv,
    as_send, as_recv, ts_send, ts_recv,
):
    clip = lax.axis_index("clip")
    cap = lax.axis_index("cap")
    rows, cols, width = shard * ncap, shard * nclip, ta_ref.shape[1]
    tiles = cols // LANE
    orders = tree_orders(nclip)
    if smat.shape != kmat.shape:
        smat = rmat

    def remote(src, dst, ss, rs, to_clip, to_cap):
        return pltpu.make_async_remote_copy(
            src_ref=src, dst_ref=dst, send_sem=ss, recv_sem=rs,
            device_id=(to_clip, to_cap), device_id_type=MESH)

    barrier = pltpu.get_barrier_semaphore()
    for j in range(1, ncap):
        pl.semaphore_signal(barrier, inc=1, device_id=(clip, lax.rem(cap + j, ncap)), device_id_type=MESH)
    for j in range(1, nclip):
        pl.semaphore_signal(barrier, inc=1, device_id=(lax.rem(clip + j, nclip), cap), device_id_type=MESH)

    for t, (a, x) in enumerate(((ta_ref, tt_ref), (sa_ref, st_ref))):
        abuf[t, cap] = a[...]
        tbuf[t, clip] = x[...]
    pl.semaphore_wait(barrier, ncap + nclip - 2)

    own_audio, own_text = (ta_ref, sa_ref), (tt_ref, st_ref)

    def tree_copy(t, mask, bit):
        src_index = flip_mask(clip, mask, nclip)
        src = own_text[t] if mask == 0 else tbuf.at[t, src_index]
        return remote(src, tbuf.at[t, src_index], tx_send.at[t, mask | bit],
                      tx_recv.at[t, mask | bit], flip(clip, bit), cap)

    def tree_forward(t, mask):
        for bit in children(mask, orders[t]):
            tree_copy(t, mask, bit).start()

    def tree_wait(t, mask):
        landed = tbuf.at[t, flip_mask(clip, mask, nclip)]
        remote(landed, landed, tx_send.at[t, mask], tx_recv.at[t, mask], clip, cap).wait_recv()

    def line_copy(t, s, step, own):
        src = own_audio[t] if own else abuf.at[t, s]
        side = 0 if step < 0 else 1
        return remote(src, abuf.at[t, s], az_send.at[t, side, s], az_recv.at[t, s], clip, cap + step)

    def line_own(t):
        @pl.when(cap + 1 < ncap)
        def _():
            line_copy(t, cap, 1, True).start()

        @pl.when(cap >= 1)
        def _():
            line_copy(t, cap, -1, True).start()

    def line_left(t, d):
        s = cap - d
        line_copy(t, s, 1, False).wait_recv()

        @pl.when(cap + 1 < ncap)
        def _():
            line_copy(t, s, 1, False).start()

    def line_right(t, d):
        s = cap + d
        line_copy(t, s, -1, False).wait_recv()

        @pl.when(cap >= 1)
        def _():
            line_copy(t, s, -1, False).start()

    def line_step(t, d):
        @pl.when(cap >= d)
        def _():
            line_left(t, d)

        @pl.when(cap + d < ncap)
        def _():
            line_right(t, d)

    step_cols = 512 if cols % 512 == 0 else LANE

    def logits(t, s):
        rs = pl.ds(pl.multiple_of(s * shard, shard), shard)
        a = abuf[t, s]
        text = tbuf.at[t].reshape(cols, width)
        top = None
        for j in range(0, cols, step_cols):
            part = 10.0 * lax.dot_general(
                a, text[j:j + step_cols, :], (((1,), (1,)), ((), ())),
                preferred_element_type=jnp.float32)
            lbuf[:, j:j + step_cols] = part
            here = jnp.max(part, axis=1, keepdims=True)
            top = here if top is None else jnp.maximum(top, here)
        total = None
        for j in range(0, cols, step_cols):
            value = jnp.exp(lbuf[:, j:j + step_cols] - top)
            if t == 0:
                kmat[rs, j:j + step_cols] = value
            else:
                smat[rs, j:j + step_cols] = value.astype(smat.dtype)
                here = jnp.sum(value, axis=1, keepdims=True)
                total = here if total is None else total + here
        wide = jnp.broadcast_to(top, (shard, LANE))
        if t == 0:
            mrep[rs, :] = wide
        else:
            smax[rs, :] = wide
            ssum[rs, :] = jnp.broadcast_to(total, (shard, LANE))

    tree_forward(0, 0)
    line_own(0)
    sequence = mask_sequence(nclip, orders[0])
    waited = 0
    for d in range(1, ncap - 1):
        amount = len(sequence) if d == ncap - 2 else min(len(sequence), waited + nclip // 2)
        if d == 1:
            line_step(0, 1)
        for mask in sequence[waited:amount]:
            tree_wait(0, mask)
            tree_forward(0, mask)
        waited = amount
        if d > 1:
            line_step(0, d)
    for mask in sequence[waited:]:
        tree_wait(0, mask)
        tree_forward(0, mask)
    tree_forward(1, 0)
    line_own(1)
    logits(0, cap)

    def early(t, d):
        @pl.when(cap >= d)
        def _():
            logits(t, cap - d)

        @pl.when(cap + d < ncap)
        def _():
            logits(t, cap + d)

    def early_loop(t, first, last):
        def one(d, carry):
            early(t, d)
            return carry
        lax.fori_loop(first, last, one, 0)

    if ncap > 1:
        def one_teacher(d, carry):
            @pl.when(d == ncap - 1)
            def _():
                if ncap > 2:
                    line_step(0, ncap - 1)
                else:
                    line_step(0, 1)
            early(0, d)
            return carry
        lax.fori_loop(1, ncap, one_teacher, 0)

    def spread(buffer, sends, recvs, k, along_cap):
        count, me = (ncap, cap) if along_cap else (nclip, clip)
        for j in range(1, count):
            peer = lax.rem(me + j, count)
            remote(buffer.at[0], buffer.at[j], sends.at[k, j], recvs.at[k, j],
                   clip if along_cap else peer, peer if along_cap else cap).start()

    def gathered(buffer, sends, recvs, k, along_cap):
        count = ncap if along_cap else nclip
        for j in range(1, count):
            copy = remote(buffer.at[0], buffer.at[j], sends.at[k, j], recvs.at[k, j], clip, cap)
            copy.wait_recv()
            copy.wait_send()

    def across(ref):
        return ref[...].T[0:1, :]

    def down(vector):
        return jnp.broadcast_to(vector, (LANE, rows)).T

    block = 64

    def column_pass():
        def one(i, carry):
            rs = pl.ds(pl.multiple_of(i * block, block), block)
            w = wrep[rs, :]
            out = []
            for t in range(tiles):
                product = kmat[rs, t * LANE:(t + 1) * LANE] * w
                out.append(carry[t] + jnp.sum(product.reshape(block // 8, 8, LANE), axis=0))
            return tuple(out)
        acc = lax.fori_loop(0, rows // block, one, tuple(jnp.zeros((8, LANE), jnp.float32) for _ in range(tiles)))
        return [jnp.sum(a, axis=0, keepdims=True) for a in acc]

    def row_pass():
        def one(i, carry):
            rs = pl.ds(pl.multiple_of(i * block, block), block)
            acc = jnp.zeros((block // 8, 8, LANE), jnp.float32)
            for t in range(tiles):
                acc = acc + kmat[rs, t * LANE:(t + 1) * LANE].reshape(block // 8, 8, LANE) * crep[:, t * LANE:(t + 1) * LANE][None]
            pbuf[rs, :] = acc.reshape(block, LANE)
            return carry
        lax.fori_loop(0, rows // block, one, 0)
        return jnp.sum(pbuf[...].T, axis=0, keepdims=True)

    student_sequence = mask_sequence(nclip, orders[1])
    half = nclip // 2

    def student_trees(masks):
        for mask in masks:
            tree_wait(1, mask)
            tree_forward(1, mask)

    def fill_max():
        student_trees(student_sequence[:half])
        if ncap > 1:
            line_step(1, 1)

    def fill_column_0():
        student_trees(student_sequence[half:])
        for d in range(2, ncap - 1):
            line_step(1, d)

    def fill_row_0():
        if ncap > 2:
            line_step(1, ncap - 1)
        logits(1, cap)

    cuts = [1, 1 + (ncap - 1) // 3, 1 + 2 * (ncap - 1) // 3, ncap]

    fills = {
        ("c", 0): fill_column_0,
        ("r", 0): fill_row_0,
        ("c", 1): lambda: early_loop(1, cuts[0], cuts[1]),
        ("r", 1): lambda: early_loop(1, cuts[1], cuts[2]),
        ("c", 2): lambda: early_loop(1, cuts[2], cuts[3]),
    }

    local_max = across(mrep)
    maxx[0] = local_max
    spread(maxx, rx_send, rx_recv, 0, True)
    fill_max()
    gathered(maxx, rx_send, rx_recv, 0, True)
    top = maxx[0]
    for j in range(1, ncap):
        top = jnp.maximum(top, maxx[j])
    factor = jnp.exp(maxx[0] - top)
    wrep[...] = down(factor)

    for it in range(ITERS):
        for t, part in enumerate(column_pass()):
            colx[it, 0, :, t * LANE:(t + 1) * LANE] = part
        spread(colx.at[it], cx_send, cx_recv, it, False)
        fills[("c", it)]()
        gathered(colx.at[it], cx_send, cx_recv, it, False)
        column = colx[it, 0]
        for j in range(1, nclip):
            column = column + colx[it, j]
        crep[...] = jnp.broadcast_to(1.0 / column, (8, cols))
        row = row_pass() * factor
        if it < ITERS - 1:
            rowx[it, 0] = row
            spread(rowx.at[it], rx_send, rx_recv, it + 1, True)
            fills[("r", it)]()
            gathered(rowx.at[it], rx_send, rx_recv, it + 1, True)
            total = rowx[it, 0]
            for j in range(1, ncap):
                total = total + rowx[it, j]
        else:
            lastx[0, 0:1, :] = row
            lastx[0, 1:2, :] = across(smax)
            lastx[0, 2:3, :] = across(ssum)
            spread(lastx, rx_send, rx_recv, it + 1, True)
            gathered(lastx, rx_send, rx_recv, it + 1, True)
            total = lastx[0, 0:1, :]
            best = lastx[0, 1:2, :]
            for j in range(1, ncap):
                total = total + lastx[j, 0:1, :]
                best = jnp.maximum(best, lastx[j, 1:2, :])
            own = jnp.exp(lastx[0, 1:2, :] - best)
            norm = own * lastx[0, 2:3, :]
            for j in range(1, ncap):
                norm = norm + jnp.exp(lastx[j, 1:2, :] - best) * lastx[j, 2:3, :]
            srep[...] = down(own / norm)
        wrep[...] = down(factor / total)

    text_student = tbuf.at[1].reshape(cols, width)

    def audio_part(i, carry):
        s = lax.rem(cap + 1 + i, ncap)
        rs = pl.ds(pl.multiple_of(s * shard, shard), shard)
        w, p = wrep[rs, :], srep[rs, :]
        for t in range(tiles):
            cs = slice(t * LANE, (t + 1) * LANE)
            target = (w * kmat[rs, cs]) * crep[0:1, cs]
            rmat[rs, cs] = (smat[rs, cs].astype(jnp.float32) * p - target).astype(jnp.bfloat16)
        grad = 10.0 * jnp.dot(rmat[rs, :], text_student[...], preferred_element_type=jnp.float32)

        @pl.when(i < ncap - 1)
        def _():
            asend[s] = grad.astype(jnp.bfloat16)
            remote(asend.at[s], arecv.at[i + 1], as_send.at[i + 1], as_recv.at[i + 1], clip, s).start()

        @pl.when(i == ncap - 1)
        def _():
            ag_ref[...] = grad
        return carry

    lax.fori_loop(0, ncap, audio_part, 0)

    group = 2 if nclip % 2 == 0 else nclip
    groups = nclip // group
    audio_student = abuf.at[1].reshape(rows, width)

    def text_part(i, carry):
        q = lax.rem(clip // group + 1 + i, groups)
        cs = pl.ds(pl.multiple_of(q * (group * shard), LANE), group * shard)
        grad = 10.0 * lax.dot_general(
            rmat[:, cs], audio_student[...], (((0,), (0,)), ((), ())),
            preferred_element_type=jnp.float32)
        for g in range(group):
            dest = q * group + g

            @pl.when(dest == clip)
            def _():
                tg_ref[...] = grad[g * shard:(g + 1) * shard, :]

            @pl.when(dest != clip)
            def _():
                offset = lax.rem(dest - clip + nclip, nclip)
                tsend[dest] = grad[g * shard:(g + 1) * shard, :].astype(jnp.bfloat16)
                remote(tsend.at[dest], trecv.at[offset], ts_send.at[offset], ts_recv.at[offset], dest, cap).start()
        return carry

    lax.fori_loop(0, groups, text_part, 0)

    for t in range(2):
        for mask in range(1, nclip):
            bit = mask & -mask
            for cand in orders[t]:
                if mask & cand:
                    bit = cand
            tree_copy(t, mask ^ bit, bit).wait_send()

        def drain(s, carry, t=t):
            @pl.when(jnp.logical_and(s <= cap, cap + 1 < ncap))
            def _():
                line_copy(t, s, 1, False).wait_send()

            @pl.when(jnp.logical_and(s >= cap, cap >= 1))
            def _():
                line_copy(t, s, -1, False).wait_send()
            return carry
        lax.fori_loop(0, ncap, drain, 0)

    for j in range(1, ncap):
        copy = remote(asend.at[0], arecv.at[j], as_send.at[j], as_recv.at[j], clip, cap)
        copy.wait_recv()
        copy.wait_send()
    total = ag_ref[...]
    for j in range(1, ncap):
        total = total + arecv[j].astype(jnp.float32)
    ag_ref[...] = total
    for j in range(1, nclip):
        copy = remote(tsend.at[0], trecv.at[j], ts_send.at[j], ts_recv.at[j], clip, cap)
        copy.wait_recv()
        copy.wait_send()
    total = tg_ref[...]
    for j in range(1, nclip):
        total = total + trecv[j].astype(jnp.float32)
    tg_ref[...] = total


def body(nclip, ncap, teacher_audio, teacher_text, student_audio, student_text):
    shard, width = teacher_audio.shape
    rows, cols = shard * ncap, shard * nclip
    f32, bf16 = jnp.float32, jnp.bfloat16
    roomy = rows * cols <= 2 ** 21
    dma = pltpu.SemaphoreType.DMA
    return pl.pallas_call(
        functools.partial(kernel, nclip, ncap, shard),
        out_shape=(jax.ShapeDtypeStruct((shard, width), f32),) * 2,
        in_specs=[pl.BlockSpec(memory_space=pltpu.VMEM)] * 4,
        out_specs=(pl.BlockSpec(memory_space=pltpu.VMEM),) * 2,
        scratch_shapes=[
            pltpu.VMEM((2, ncap, shard, width), bf16),
            pltpu.VMEM((2, nclip, shard, width), bf16),
            pltpu.VMEM((rows, cols), f32),
            pltpu.VMEM((rows, cols) if roomy else (8, LANE), f32),
            pltpu.VMEM((rows, cols), bf16),
            pltpu.VMEM((shard, cols), f32),
            pltpu.VMEM((rows, LANE), f32),
            pltpu.VMEM((rows, LANE), f32),
            pltpu.VMEM((rows, LANE), f32),
            pltpu.VMEM((8, cols), f32),
            pltpu.VMEM((rows, LANE), f32),
            pltpu.VMEM((rows, LANE), f32),
            pltpu.VMEM((rows, LANE), f32),
            pltpu.VMEM((ITERS, ncap, 1, rows), f32),
            pltpu.VMEM((ITERS, nclip, 1, cols), f32),
            pltpu.VMEM((ncap, 1, rows), f32),
            pltpu.VMEM((ncap, 3, rows), f32),
            pltpu.VMEM((ncap, shard, width), bf16),
            pltpu.VMEM((ncap, shard, width), bf16),
            pltpu.VMEM((nclip, shard, width), bf16),
            pltpu.VMEM((nclip, shard, width), bf16),
            dma((2, 2, ncap)), dma((2, ncap)),
            dma((2, nclip)), dma((2, nclip)),
            dma((ITERS + 1, ncap)), dma((ITERS + 1, ncap)),
            dma((ITERS, nclip)), dma((ITERS, nclip)),
            dma((ncap,)), dma((ncap,)),
            dma((nclip,)), dma((nclip,)),
        ],
        compiler_params=pltpu.CompilerParams(
            collective_id=0, has_side_effects=True, vmem_limit_bytes=66 * 1000 * 1000),
    )(teacher_audio, teacher_text, student_audio, student_text)


def solution(mesh):
    nclip, ncap = mesh.shape["clip"], mesh.shape["cap"]
    placed = (
        P(("clip", "cap"), None),
        P(("cap", "clip"), None),
        P(("clip", "cap"), None),
        P(("cap", "clip"), None),
    )
    return jax.shard_map(
        functools.partial(body, nclip, ncap),
        mesh=mesh,
        in_specs=placed,
        out_specs=(P(("clip", "cap"), None), P(("cap", "clip"), None)),
        check_vma=False,
    )
```

```python
import functools

import jax
import jax.numpy as jnp
from jax import lax
from jax.experimental import pallas as pl
from jax.experimental.pallas import tpu as pltpu
from jax.sharding import PartitionSpec as P

ITERS = 3
LANE = 128
MESH = pl.DeviceIdType.MESH


def flip(index, bit):
    return index + bit * (1 - 2 * ((index // bit) % 2))


def flip_mask(index, mask, count):
    bit = 1
    while bit < count:
        if mask & bit:
            index = flip(index, bit)
        bit *= 2
    return index


def tree_orders(count):
    bits = []
    bit = 2
    while bit < count:
        bits.append(bit)
        bit *= 2
    tail = [1] if count > 1 else []
    return (bits + tail, bits[::-1] + tail)


def children(mask, order):
    last = -1
    for position, bit in enumerate(order):
        if mask & bit:
            last = position
    return [bit for bit in order[last + 1:]]


def mask_sequence(count, order):
    out, level = [], [0]
    while level:
        following = []
        for mask in level:
            for bit in children(mask, order):
                following.append(mask | bit)
        out.extend(following)
        level = following
    return out


def kernel(
    nclip, ncap, shard,
    ta_ref, tt_ref, sa_ref, st_ref, ag_ref, tg_ref,
    abuf, tbuf, kmat, smat, rmat, lbuf, pbuf, wrep, srep, crep, mrep, smax, ssum,
    rowx, colx, maxx, lastx, akeep, asend, arecv, tkeep, psend, precv, tsend, trecv,
    az_send, az_recv, tx_send, tx_recv, rx_send, rx_recv, cx_send, cx_recv,
    as_send, as_recv, ps_send, ps_recv, ts_send, ts_recv,
):
    clip = lax.axis_index("clip")
    cap = lax.axis_index("cap")
    rows, cols, width = shard * ncap, shard * nclip, ta_ref.shape[1]
    tiles = cols // LANE
    orders = tree_orders(nclip)
    if smat.shape != kmat.shape:
        smat = rmat

    def remote(src, dst, ss, rs, to_clip, to_cap):
        return pltpu.make_async_remote_copy(
            src_ref=src, dst_ref=dst, send_sem=ss, recv_sem=rs,
            device_id=(to_clip, to_cap), device_id_type=MESH)

    barrier = pltpu.get_barrier_semaphore()
    for j in range(1, ncap):
        pl.semaphore_signal(barrier, inc=1, device_id=(clip, lax.rem(cap + j, ncap)), device_id_type=MESH)
    for j in range(1, nclip):
        pl.semaphore_signal(barrier, inc=1, device_id=(lax.rem(clip + j, nclip), cap), device_id_type=MESH)

    for t, (a, x) in enumerate(((ta_ref, tt_ref), (sa_ref, st_ref))):
        abuf[t, cap] = a[...]
        tbuf[t, clip] = x[...]
    pl.semaphore_wait(barrier, ncap + nclip - 2)

    own_audio, own_text = (ta_ref, sa_ref), (tt_ref, st_ref)

    def tree_copy(t, mask, bit):
        src_index = flip_mask(clip, mask, nclip)
        src = own_text[t] if mask == 0 else tbuf.at[t, src_index]
        return remote(src, tbuf.at[t, src_index], tx_send.at[t, mask | bit],
                      tx_recv.at[t, mask | bit], flip(clip, bit), cap)

    def tree_forward(t, mask):
        for bit in children(mask, orders[t]):
            tree_copy(t, mask, bit).start()

    def tree_wait(t, mask):
        landed = tbuf.at[t, flip_mask(clip, mask, nclip)]
        remote(landed, landed, tx_send.at[t, mask], tx_recv.at[t, mask], clip, cap).wait_recv()

    def line_copy(t, s, step, own):
        src = own_audio[t] if own else abuf.at[t, s]
        side = 0 if step < 0 else 1
        return remote(src, abuf.at[t, s], az_send.at[t, side, s], az_recv.at[t, s], clip, cap + step)

    def line_own(t):
        @pl.when(cap + 1 < ncap)
        def _():
            line_copy(t, cap, 1, True).start()

        @pl.when(cap >= 1)
        def _():
            line_copy(t, cap, -1, True).start()

    def line_left(t, d):
        s = cap - d
        line_copy(t, s, 1, False).wait_recv()

        @pl.when(cap + 1 < ncap)
        def _():
            line_copy(t, s, 1, False).start()

    def line_right(t, d):
        s = cap + d
        line_copy(t, s, -1, False).wait_recv()

        @pl.when(cap >= 1)
        def _():
            line_copy(t, s, -1, False).start()

    def line_step(t, d):
        @pl.when(cap >= d)
        def _():
            line_left(t, d)

        @pl.when(cap + d < ncap)
        def _():
            line_right(t, d)

    step_cols = 512 if cols % 512 == 0 else LANE

    def logits(t, s):
        rs = pl.ds(pl.multiple_of(s * shard, shard), shard)
        a = abuf[t, s]
        text = tbuf.at[t].reshape(cols, width)
        top = None
        for j in range(0, cols, step_cols):
            part = 10.0 * lax.dot_general(
                a, text[j:j + step_cols, :], (((1,), (1,)), ((), ())),
                preferred_element_type=jnp.float32)
            lbuf[:, j:j + step_cols] = part
            here = jnp.max(part, axis=1, keepdims=True)
            top = here if top is None else jnp.maximum(top, here)
        total = None
        for j in range(0, cols, step_cols):
            value = jnp.exp(lbuf[:, j:j + step_cols] - top)
            if t == 0:
                kmat[rs, j:j + step_cols] = value
            else:
                smat[rs, j:j + step_cols] = value.astype(smat.dtype)
                here = jnp.sum(value, axis=1, keepdims=True)
                total = here if total is None else total + here
        wide = jnp.broadcast_to(top, (shard, LANE))
        if t == 0:
            mrep[rs, :] = wide
        else:
            smax[rs, :] = wide
            ssum[rs, :] = jnp.broadcast_to(total, (shard, LANE))

    tree_forward(0, 0)
    line_own(0)
    sequence = mask_sequence(nclip, orders[0])
    waited = 0
    for d in range(1, ncap - 1):
        amount = len(sequence) if d == ncap - 2 else min(len(sequence), waited + nclip // 2)
        if d == 1:
            line_step(0, 1)
        for mask in sequence[waited:amount]:
            tree_wait(0, mask)
            tree_forward(0, mask)
        waited = amount
        if d > 1:
            line_step(0, d)
    for mask in sequence[waited:]:
        tree_wait(0, mask)
        tree_forward(0, mask)
    tree_forward(1, 0)
    line_own(1)
    logits(0, cap)

    def early(t, d):
        @pl.when(cap >= d)
        def _():
            logits(t, cap - d)

        @pl.when(cap + d < ncap)
        def _():
            logits(t, cap + d)

    def early_loop(t, first, last):
        def one(d, carry):
            early(t, d)
            return carry
        lax.fori_loop(first, last, one, 0)

    if ncap > 1:
        def one_teacher(d, carry):
            @pl.when(d == ncap - 1)
            def _():
                if ncap > 2:
                    line_step(0, ncap - 1)
                else:
                    line_step(0, 1)
            early(0, d)
            return carry
        lax.fori_loop(1, ncap, one_teacher, 0)

    def spread(buffer, sends, recvs, k, along_cap):
        count, me = (ncap, cap) if along_cap else (nclip, clip)
        for j in range(1, count):
            peer = lax.rem(me + j, count)
            remote(buffer.at[0], buffer.at[j], sends.at[k, j], recvs.at[k, j],
                   clip if along_cap else peer, peer if along_cap else cap).start()

    def gathered(buffer, sends, recvs, k, along_cap):
        count = ncap if along_cap else nclip
        for j in range(1, count):
            copy = remote(buffer.at[0], buffer.at[j], sends.at[k, j], recvs.at[k, j], clip, cap)
            copy.wait_recv()
            copy.wait_send()

    def across(ref):
        return ref[...].T[0:1, :]

    def down(vector):
        return jnp.broadcast_to(vector, (LANE, rows)).T

    block = 64

    def column_pass():
        def one(i, carry):
            rs = pl.ds(pl.multiple_of(i * block, block), block)
            w = wrep[rs, :]
            out = []
            for t in range(tiles):
                product = kmat[rs, t * LANE:(t + 1) * LANE] * w
                out.append(carry[t] + jnp.sum(product.reshape(block // 8, 8, LANE), axis=0))
            return tuple(out)
        acc = lax.fori_loop(0, rows // block, one, tuple(jnp.zeros((8, LANE), jnp.float32) for _ in range(tiles)))
        return [jnp.sum(a, axis=0, keepdims=True) for a in acc]

    def row_pass():
        def one(i, carry):
            rs = pl.ds(pl.multiple_of(i * block, block), block)
            acc = jnp.zeros((block // 8, 8, LANE), jnp.float32)
            for t in range(tiles):
                acc = acc + kmat[rs, t * LANE:(t + 1) * LANE].reshape(block // 8, 8, LANE) * crep[:, t * LANE:(t + 1) * LANE][None]
            pbuf[rs, :] = acc.reshape(block, LANE)
            return carry
        lax.fori_loop(0, rows // block, one, 0)
        return jnp.sum(pbuf[...].T, axis=0, keepdims=True)

    student_sequence = mask_sequence(nclip, orders[1])
    half = nclip // 2

    def student_trees(masks):
        for mask in masks:
            tree_wait(1, mask)
            tree_forward(1, mask)

    def fill_max():
        student_trees(student_sequence[:half])
        if ncap > 1:
            line_step(1, 1)

    def fill_column_0():
        student_trees(student_sequence[half:])
        for d in range(2, ncap - 1):
            line_step(1, d)

    def fill_row_0():
        if ncap > 2:
            line_step(1, ncap - 1)
        logits(1, cap)

    cuts = [1, 1 + (ncap - 1) // 3, 1 + 2 * (ncap - 1) // 3, ncap]

    fills = {
        ("c", 0): fill_column_0,
        ("r", 0): fill_row_0,
        ("c", 1): lambda: early_loop(1, cuts[0], cuts[1]),
        ("r", 1): lambda: early_loop(1, cuts[1], cuts[2]),
        ("c", 2): lambda: early_loop(1, cuts[2], cuts[3]),
    }

    local_max = across(mrep)
    maxx[0] = local_max
    spread(maxx, rx_send, rx_recv, 0, True)
    fill_max()
    gathered(maxx, rx_send, rx_recv, 0, True)
    top = maxx[0]
    for j in range(1, ncap):
        top = jnp.maximum(top, maxx[j])
    factor = jnp.exp(maxx[0] - top)
    wrep[...] = down(factor)

    for it in range(ITERS):
        for t, part in enumerate(column_pass()):
            colx[it, 0, :, t * LANE:(t + 1) * LANE] = part
        spread(colx.at[it], cx_send, cx_recv, it, False)
        fills[("c", it)]()
        gathered(colx.at[it], cx_send, cx_recv, it, False)
        column = colx[it, 0]
        for j in range(1, nclip):
            column = column + colx[it, j]
        crep[...] = jnp.broadcast_to(1.0 / column, (8, cols))
        row = row_pass() * factor
        if it < ITERS - 1:
            rowx[it, 0] = row
            spread(rowx.at[it], rx_send, rx_recv, it + 1, True)
            fills[("r", it)]()
            gathered(rowx.at[it], rx_send, rx_recv, it + 1, True)
            total = rowx[it, 0]
            for j in range(1, ncap):
                total = total + rowx[it, j]
        else:
            lastx[0, 0:1, :] = row
            lastx[0, 1:2, :] = across(smax)
            lastx[0, 2:3, :] = across(ssum)
            spread(lastx, rx_send, rx_recv, it + 1, True)
            gathered(lastx, rx_send, rx_recv, it + 1, True)
            total = lastx[0, 0:1, :]
            best = lastx[0, 1:2, :]
            for j in range(1, ncap):
                total = total + lastx[j, 0:1, :]
                best = jnp.maximum(best, lastx[j, 1:2, :])
            own = jnp.exp(lastx[0, 1:2, :] - best)
            norm = own * lastx[0, 2:3, :]
            for j in range(1, ncap):
                norm = norm + jnp.exp(lastx[j, 1:2, :] - best) * lastx[j, 2:3, :]
            srep[...] = down(own / norm)
        wrep[...] = down(factor / total)

    text_student = tbuf.at[1].reshape(cols, width)
    half_rows = shard // 2

    def line_sum_copy(s, h, slot, step):
        return remote(asend.at[s, h], arecv.at[slot, h], as_send.at[s, h], as_recv.at[slot, h], clip, cap + step)

    def landed(slot, h):
        here = arecv.at[slot, h]
        remote(here, here, as_send.at[0, h], as_recv.at[slot, h], clip, cap).wait_recv()

    def audio_part(s):
        rs = pl.ds(pl.multiple_of(s * shard, shard), shard)
        w, p = wrep[rs, :], srep[rs, :]
        for t in range(tiles):
            cs = slice(t * LANE, (t + 1) * LANE)
            target = (w * kmat[rs, cs]) * crep[0:1, cs]
            rmat[rs, cs] = (smat[rs, cs].astype(jnp.float32) * p - target).astype(jnp.bfloat16)
        grad = 10.0 * jnp.dot(rmat[rs, :], text_student[...], preferred_element_type=jnp.float32)
        for h in range(2):
            akeep[s, h] = grad[h * half_rows:(h + 1) * half_rows, :]

    def first_send(s, slot, step):
        for h in range(2):
            asend[s, h] = akeep[s, h].astype(jnp.bfloat16)
            line_sum_copy(s, h, slot, step).start()

    def left_slot(s, d):
        return s + (ncap - s) * (1 // d)

    def audio_parts(i, carry):
        d = ncap - 1 - i

        @pl.when(cap + d < ncap)
        def _():
            s = cap + d
            audio_part(s)

            @pl.when(cap == 0)
            def _():
                first_send(s, s, 1)

        @pl.when(cap >= d)
        def _():
            s = cap - d
            audio_part(s)

            @pl.when(cap == ncap - 1)
            def _():
                first_send(s, left_slot(s, d), -1)
        return carry

    lax.fori_loop(0, ncap - 1, audio_parts, 0)
    audio_part(cap)

    def relay_one(s, h, slot, step):
        landed(s, h)
        asend[s, h] = (akeep[s, h] + arecv[s, h].astype(jnp.float32)).astype(jnp.bfloat16)
        line_sum_copy(s, h, slot, step).start()

    def relay(d):
        for h in range(2):
            @pl.when(jnp.logical_and(cap >= 1, cap + d < ncap))
            def _():
                relay_one(cap + d, h, cap + d, 1)

            @pl.when(jnp.logical_and(cap + 1 < ncap, cap >= d))
            def _():
                s = cap - d
                relay_one(s, h, left_slot(s, d), -1)

    groups = nclip // 2
    chip, parity = clip // 2, clip % 2
    audio_student = abuf.at[1].reshape(rows, width)

    def pair_copy(q):
        return remote(psend.at[q], precv.at[q], ps_send.at[q], ps_recv.at[q], flip(clip, 1), cap)

    def text_copy(q, offset):
        return remote(tsend.at[q], trecv.at[offset], ts_send.at[offset], ts_recv.at[offset], q * 2 + parity, cap)

    def text_step(i, carry):
        @pl.when(i < groups)
        def _():
            q = (chip + 1 + i) % groups
            cs = pl.ds(pl.multiple_of(q * (2 * shard), LANE), 2 * shard)
            grad = 10.0 * lax.dot_general(
                rmat[:, cs], audio_student[...], (((0,), (0,)), ((), ())),
                preferred_element_type=jnp.float32)
            for g in range(2):
                @pl.when(parity == g)
                def _():
                    psend[q] = grad[(1 - g) * shard:(2 - g) * shard, :].astype(jnp.bfloat16)
                    tkeep[q] = grad[g * shard:(g + 1) * shard, :]
            pair_copy(q).start()

        @pl.when(i >= 1)
        def _():
            q = (chip + i) % groups
            pair_copy(q).wait_recv()
            both = tkeep[q] + precv[q].astype(jnp.float32)

            @pl.when(i < groups)
            def _():
                tsend[q] = both.astype(jnp.bfloat16)
                text_copy(q, i).start()

            @pl.when(i == groups)
            def _():
                tg_ref[...] = both
        return carry

    middle = max(groups // 2, 1)
    lax.fori_loop(0, middle, text_step, 0)

    def relays(i, carry):
        relay(ncap - 2 - i)
        return carry

    lax.fori_loop(0, ncap - 3, relays, 0)
    lax.fori_loop(middle, groups + 1, text_step, 0)
    if ncap > 2:
        relay(1)

    for t in range(2):
        for mask in range(1, nclip):
            bit = mask & -mask
            for cand in orders[t]:
                if mask & cand:
                    bit = cand
            tree_copy(t, mask ^ bit, bit).wait_send()

        def drain(s, carry, t=t):
            @pl.when(jnp.logical_and(s <= cap, cap + 1 < ncap))
            def _():
                line_copy(t, s, 1, False).wait_send()

            @pl.when(jnp.logical_and(s >= cap, cap >= 1))
            def _():
                line_copy(t, s, -1, False).wait_send()
            return carry
        lax.fori_loop(0, ncap, drain, 0)

    def drain_sums(s, carry):
        @pl.when(s != cap)
        def _():
            for h in range(2):
                line_sum_copy(s, h, s, 0).wait_send()
        return carry
    lax.fori_loop(0, ncap, drain_sums, 0)

    def drain_pairs(q, carry):
        pair_copy(q).wait_send()
        return carry
    lax.fori_loop(0, groups, drain_pairs, 0)

    total = tg_ref[...]
    for j in range(1, groups):
        copy = text_copy(chip, j)
        copy.wait_recv()
        copy.wait_send()
        total = total + trecv[j].astype(jnp.float32)
    tg_ref[...] = total

    for h in range(2):
        ag_ref[h * half_rows:(h + 1) * half_rows, :] = akeep[cap, h]

        def add(slot, h=h):
            landed(slot, h)
            ag_ref[h * half_rows:(h + 1) * half_rows, :] += arecv[slot, h].astype(jnp.float32)

        @pl.when(cap >= 1)
        def _():
            add(cap)

        @pl.when(cap + 1 < ncap)
        def _():
            add(ncap)


def body(nclip, ncap, teacher_audio, teacher_text, student_audio, student_text):
    shard, width = teacher_audio.shape
    rows, cols = shard * ncap, shard * nclip
    f32, bf16 = jnp.float32, jnp.bfloat16
    roomy = rows * cols <= 2 ** 21
    dma = pltpu.SemaphoreType.DMA
    return pl.pallas_call(
        functools.partial(kernel, nclip, ncap, shard),
        out_shape=(jax.ShapeDtypeStruct((shard, width), f32),) * 2,
        in_specs=[pl.BlockSpec(memory_space=pltpu.VMEM)] * 4,
        out_specs=(pl.BlockSpec(memory_space=pltpu.VMEM),) * 2,
        scratch_shapes=[
            pltpu.VMEM((2, ncap, shard, width), bf16),
            pltpu.VMEM((2, nclip, shard, width), bf16),
            pltpu.VMEM((rows, cols), f32),
            pltpu.VMEM((rows, cols) if roomy else (8, LANE), f32),
            pltpu.VMEM((rows, cols), bf16),
            pltpu.VMEM((shard, cols), f32),
            pltpu.VMEM((rows, LANE), f32),
            pltpu.VMEM((rows, LANE), f32),
            pltpu.VMEM((rows, LANE), f32),
            pltpu.VMEM((8, cols), f32),
            pltpu.VMEM((rows, LANE), f32),
            pltpu.VMEM((rows, LANE), f32),
            pltpu.VMEM((rows, LANE), f32),
            pltpu.VMEM((ITERS, ncap, 1, rows), f32),
            pltpu.VMEM((ITERS, nclip, 1, cols), f32),
            pltpu.VMEM((ncap, 1, rows), f32),
            pltpu.VMEM((ncap, 3, rows), f32),
            pltpu.VMEM((ncap, 2, shard // 2, width), f32),
            pltpu.VMEM((ncap, 2, shard // 2, width), bf16),
            pltpu.VMEM((ncap + 1, 2, shard // 2, width), bf16),
            pltpu.VMEM((nclip // 2, shard, width), f32),
            pltpu.VMEM((nclip // 2, shard, width), bf16),
            pltpu.VMEM((nclip // 2, shard, width), bf16),
            pltpu.VMEM((nclip // 2, shard, width), bf16),
            pltpu.VMEM((nclip // 2, shard, width), bf16),
            dma((2, 2, ncap)), dma((2, ncap)),
            dma((2, nclip)), dma((2, nclip)),
            dma((ITERS + 1, ncap)), dma((ITERS + 1, ncap)),
            dma((ITERS, nclip)), dma((ITERS, nclip)),
            dma((ncap, 2)), dma((ncap + 1, 2)),
            dma((nclip // 2,)), dma((nclip // 2,)),
            dma((nclip // 2,)), dma((nclip // 2,)),
        ],
        compiler_params=pltpu.CompilerParams(
            collective_id=0, has_side_effects=True, vmem_limit_bytes=66 * 1000 * 1000),
    )(teacher_audio, teacher_text, student_audio, student_text)


def solution(mesh):
    nclip, ncap = mesh.shape["clip"], mesh.shape["cap"]
    placed = (
        P(("clip", "cap"), None),
        P(("cap", "clip"), None),
        P(("clip", "cap"), None),
        P(("cap", "clip"), None),
    )
    return jax.shard_map(
        functools.partial(body, nclip, ncap),
        mesh=mesh,
        in_specs=placed,
        out_specs=(P(("clip", "cap"), None), P(("cap", "clip"), None)),
        check_vma=False,
    )
```

```python
import functools

import jax
import jax.numpy as jnp
from jax import lax
from jax.experimental import pallas as pl
from jax.experimental.pallas import tpu as pltpu
from jax.sharding import PartitionSpec as P

ITERS = 3
LANE = 128
MESH = pl.DeviceIdType.MESH


def flip(index, bit):
    return index + bit * (1 - 2 * ((index // bit) % 2))


def flip_mask(index, mask, count):
    bit = 1
    while bit < count:
        if mask & bit:
            index = flip(index, bit)
        bit *= 2
    return index


def tree_orders(count):
    bits = []
    bit = 2
    while bit < count:
        bits.append(bit)
        bit *= 2
    tail = [1] if count > 1 else []
    return (bits + tail, bits[::-1] + tail)


def children(mask, order):
    last = -1
    for position, bit in enumerate(order):
        if mask & bit:
            last = position
    return [bit for bit in order[last + 1:]]


def mask_sequence(count, order):
    out, level = [], [0]
    while level:
        following = []
        for mask in level:
            for bit in children(mask, order):
                following.append(mask | bit)
        out.extend(following)
        level = following
    return out


def kernel(
    nclip, ncap, shard,
    ta_ref, tt_ref, sa_ref, st_ref, ag_ref, tg_ref,
    abuf, tbuf, kmat, smat, rmat, lbuf, pbuf, wrep, srep, crep, mrep, smax, ssum,
    rowx, colx, maxx, lastx, akeep, asend, arecv, tkeep, psend, precv, tsend, trecv,
    az_send, az_recv, tx_send, tx_recv, rx_send, rx_recv, cx_send, cx_recv,
    as_send, as_recv, ps_send, ps_recv, ts_send, ts_recv,
):
    clip = lax.axis_index("clip")
    cap = lax.axis_index("cap")
    rows, cols, width = shard * ncap, shard * nclip, ta_ref.shape[1]
    tiles = cols // LANE
    orders = tree_orders(nclip)
    if smat.shape != kmat.shape:
        smat = rmat

    def remote(src, dst, ss, rs, to_clip, to_cap):
        return pltpu.make_async_remote_copy(
            src_ref=src, dst_ref=dst, send_sem=ss, recv_sem=rs,
            device_id=(to_clip, to_cap), device_id_type=MESH)

    barrier = pltpu.get_barrier_semaphore()
    for j in range(1, ncap):
        pl.semaphore_signal(barrier, inc=1, device_id=(clip, lax.rem(cap + j, ncap)), device_id_type=MESH)
    for j in range(1, nclip):
        pl.semaphore_signal(barrier, inc=1, device_id=(lax.rem(clip + j, nclip), cap), device_id_type=MESH)

    for t, (a, x) in enumerate(((ta_ref, tt_ref), (sa_ref, st_ref))):
        abuf[t, cap] = a[...]
        tbuf[t, clip] = x[...]
    pl.semaphore_wait(barrier, ncap + nclip - 2)

    own_audio, own_text = (ta_ref, sa_ref), (tt_ref, st_ref)

    def tree_copy(t, mask, bit):
        src_index = flip_mask(clip, mask, nclip)
        src = own_text[t] if mask == 0 else tbuf.at[t, src_index]
        return remote(src, tbuf.at[t, src_index], tx_send.at[t, mask | bit],
                      tx_recv.at[t, mask | bit], flip(clip, bit), cap)

    def tree_forward(t, mask):
        for bit in children(mask, orders[t]):
            tree_copy(t, mask, bit).start()

    def tree_wait(t, mask):
        landed = tbuf.at[t, flip_mask(clip, mask, nclip)]
        remote(landed, landed, tx_send.at[t, mask], tx_recv.at[t, mask], clip, cap).wait_recv()

    def line_copy(t, s, h, step, own):
        part = pl.ds(h * (shard // 2), shard // 2)
        dst = abuf.at[t, s, part, :]
        src = own_audio[t].at[part, :] if own else dst
        side = 0 if step < 0 else 1
        return remote(src, dst, az_send.at[t, side, s, h], az_recv.at[t, s, h], clip, cap + step)

    def line_own(t):
        for h in range(2):
            @pl.when(cap + 1 < ncap)
            def _():
                line_copy(t, cap, h, 1, True).start()

            @pl.when(cap >= 1)
            def _():
                line_copy(t, cap, h, -1, True).start()

    def line_left(t, d, h):
        s = cap - d
        line_copy(t, s, h, 1, False).wait_recv()

        @pl.when(cap + 1 < ncap)
        def _():
            line_copy(t, s, h, 1, False).start()

    def line_right(t, d, h):
        s = cap + d
        line_copy(t, s, h, -1, False).wait_recv()

        @pl.when(cap >= 1)
        def _():
            line_copy(t, s, h, -1, False).start()

    def line_step(t, d):
        for h in range(2):
            @pl.when(cap >= d)
            def _():
                line_left(t, d, h)

            @pl.when(cap + d < ncap)
            def _():
                line_right(t, d, h)

    step_cols = 512 if cols % 512 == 0 else LANE

    def logits(t, s):
        rs = pl.ds(pl.multiple_of(s * shard, shard), shard)
        a = abuf[t, s]
        text = tbuf.at[t].reshape(cols, width)
        top = None
        for j in range(0, cols, step_cols):
            part = 10.0 * lax.dot_general(
                a, text[j:j + step_cols, :], (((1,), (1,)), ((), ())),
                preferred_element_type=jnp.float32)
            lbuf[:, j:j + step_cols] = part
            here = jnp.max(part, axis=1, keepdims=True)
            top = here if top is None else jnp.maximum(top, here)
        total = None
        for j in range(0, cols, step_cols):
            value = jnp.exp(lbuf[:, j:j + step_cols] - top)
            if t == 0:
                kmat[rs, j:j + step_cols] = value
            else:
                smat[rs, j:j + step_cols] = value.astype(smat.dtype)
                here = jnp.sum(value, axis=1, keepdims=True)
                total = here if total is None else total + here
        wide = jnp.broadcast_to(top, (shard, LANE))
        if t == 0:
            mrep[rs, :] = wide
        else:
            smax[rs, :] = wide
            ssum[rs, :] = jnp.broadcast_to(total, (shard, LANE))

    tree_forward(0, 0)
    line_own(0)
    sequence = mask_sequence(nclip, orders[0])
    waited = len(orders[0])
    if ncap > 2:
        line_step(0, 1)
    for mask in sequence[:waited]:
        tree_wait(0, mask)
        tree_forward(0, mask)
    for d in range(2, ncap - 1):
        line_step(0, d)
    for mask in sequence[waited:]:
        tree_wait(0, mask)
        tree_forward(0, mask)
    tree_forward(1, 0)
    line_own(1)
    logits(0, cap)

    def early(t, d):
        @pl.when(cap >= d)
        def _():
            logits(t, cap - d)

        @pl.when(cap + d < ncap)
        def _():
            logits(t, cap + d)

    def early_loop(t, first, last):
        def one(d, carry):
            early(t, d)
            return carry
        lax.fori_loop(first, last, one, 0)

    if ncap > 1:
        def one_teacher(d, carry):
            @pl.when(d == ncap - 1)
            def _():
                if ncap > 2:
                    line_step(0, ncap - 1)
                else:
                    line_step(0, 1)
            early(0, d)
            return carry
        lax.fori_loop(1, ncap, one_teacher, 0)

    def spread(buffer, sends, recvs, k, along_cap):
        count, me = (ncap, cap) if along_cap else (nclip, clip)
        for j in range(1, count):
            peer = lax.rem(me + j, count)
            remote(buffer.at[0], buffer.at[j], sends.at[k, j], recvs.at[k, j],
                   clip if along_cap else peer, peer if along_cap else cap).start()

    def gathered(buffer, sends, recvs, k, along_cap):
        count = ncap if along_cap else nclip
        for j in range(1, count):
            copy = remote(buffer.at[0], buffer.at[j], sends.at[k, j], recvs.at[k, j], clip, cap)
            copy.wait_recv()
            copy.wait_send()

    def across(ref):
        return ref[...].T[0:1, :]

    def down(vector):
        return jnp.broadcast_to(vector, (LANE, rows)).T

    block = 64

    def column_pass():
        def one(i, carry):
            rs = pl.ds(pl.multiple_of(i * block, block), block)
            w = wrep[rs, :]
            out = []
            for t in range(tiles):
                product = kmat[rs, t * LANE:(t + 1) * LANE] * w
                out.append(carry[t] + jnp.sum(product.reshape(block // 8, 8, LANE), axis=0))
            return tuple(out)
        acc = lax.fori_loop(0, rows // block, one, tuple(jnp.zeros((8, LANE), jnp.float32) for _ in range(tiles)))
        return [jnp.sum(a, axis=0, keepdims=True) for a in acc]

    def row_pass():
        def one(i, carry):
            rs = pl.ds(pl.multiple_of(i * block, block), block)
            acc = jnp.zeros((block // 8, 8, LANE), jnp.float32)
            for t in range(tiles):
                acc = acc + kmat[rs, t * LANE:(t + 1) * LANE].reshape(block // 8, 8, LANE) * crep[:, t * LANE:(t + 1) * LANE][None]
            pbuf[rs, :] = acc.reshape(block, LANE)
            return carry
        lax.fori_loop(0, rows // block, one, 0)
        return jnp.sum(pbuf[...].T, axis=0, keepdims=True)

    student_sequence = mask_sequence(nclip, orders[1])
    half = nclip // 2

    def student_trees(masks):
        for mask in masks:
            tree_wait(1, mask)
            tree_forward(1, mask)

    def fill_max():
        student_trees(student_sequence[:half])
        if ncap > 1:
            line_step(1, 1)

    def fill_column_0():
        student_trees(student_sequence[half:])
        for d in range(2, ncap - 1):
            line_step(1, d)

    def fill_row_0():
        if ncap > 2:
            line_step(1, ncap - 1)
        logits(1, cap)

    cuts = [1, 1 + (ncap - 1) // 3, 1 + 2 * (ncap - 1) // 3, ncap]

    fills = {
        ("c", 0): fill_column_0,
        ("r", 0): fill_row_0,
        ("c", 1): lambda: early_loop(1, cuts[0], cuts[1]),
        ("r", 1): lambda: early_loop(1, cuts[1], cuts[2]),
        ("c", 2): lambda: early_loop(1, cuts[2], cuts[3]),
    }

    local_max = across(mrep)
    maxx[0] = local_max
    spread(maxx, rx_send, rx_recv, 0, True)
    fill_max()
    gathered(maxx, rx_send, rx_recv, 0, True)
    top = maxx[0]
    for j in range(1, ncap):
        top = jnp.maximum(top, maxx[j])
    factor = jnp.exp(maxx[0] - top)
    wrep[...] = down(factor)

    for it in range(ITERS):
        for t, part in enumerate(column_pass()):
            colx[it, 0, :, t * LANE:(t + 1) * LANE] = part
        spread(colx.at[it], cx_send, cx_recv, it, False)
        fills[("c", it)]()
        gathered(colx.at[it], cx_send, cx_recv, it, False)
        column = colx[it, 0]
        for j in range(1, nclip):
            column = column + colx[it, j]
        crep[...] = jnp.broadcast_to(1.0 / column, (8, cols))
        row = row_pass() * factor
        if it < ITERS - 1:
            rowx[it, 0] = row
            spread(rowx.at[it], rx_send, rx_recv, it + 1, True)
            fills[("r", it)]()
            gathered(rowx.at[it], rx_send, rx_recv, it + 1, True)
            total = rowx[it, 0]
            for j in range(1, ncap):
                total = total + rowx[it, j]
        else:
            lastx[0, 0:1, :] = row
            lastx[0, 1:2, :] = across(smax)
            lastx[0, 2:3, :] = across(ssum)
            spread(lastx, rx_send, rx_recv, it + 1, True)
            gathered(lastx, rx_send, rx_recv, it + 1, True)
            total = lastx[0, 0:1, :]
            best = lastx[0, 1:2, :]
            for j in range(1, ncap):
                total = total + lastx[j, 0:1, :]
                best = jnp.maximum(best, lastx[j, 1:2, :])
            own = jnp.exp(lastx[0, 1:2, :] - best)
            norm = own * lastx[0, 2:3, :]
            for j in range(1, ncap):
                norm = norm + jnp.exp(lastx[j, 1:2, :] - best) * lastx[j, 2:3, :]
            srep[...] = down(own / norm)
        wrep[...] = down(factor / total)

    text_student = tbuf.at[1].reshape(cols, width)
    half_rows = shard // 2

    def line_sum_copy(s, h, slot, step):
        return remote(asend.at[s, h], arecv.at[slot, h], as_send.at[s, h], as_recv.at[slot, h], clip, cap + step)

    def landed(slot, h):
        here = arecv.at[slot, h]
        remote(here, here, as_send.at[0, h], as_recv.at[slot, h], clip, cap).wait_recv()

    def audio_part(s):
        rs = pl.ds(pl.multiple_of(s * shard, shard), shard)
        w, p = wrep[rs, :], srep[rs, :]
        for t in range(tiles):
            cs = slice(t * LANE, (t + 1) * LANE)
            target = (w * kmat[rs, cs]) * crep[0:1, cs]
            rmat[rs, cs] = (smat[rs, cs].astype(jnp.float32) * p - target).astype(jnp.bfloat16)
        grad = 10.0 * jnp.dot(rmat[rs, :], text_student[...], preferred_element_type=jnp.float32)
        for h in range(2):
            akeep[s, h] = grad[h * half_rows:(h + 1) * half_rows, :]

    def first_send(s, slot, step):
        for h in range(2):
            asend[s, h] = akeep[s, h].astype(jnp.bfloat16)
            line_sum_copy(s, h, slot, step).start()

    def left_slot(s, d):
        return s + (ncap - s) * (1 // d)

    def audio_parts(i, carry):
        d = ncap - 1 - i

        @pl.when(cap + d < ncap)
        def _():
            s = cap + d
            audio_part(s)

            @pl.when(cap == 0)
            def _():
                first_send(s, s, 1)

        @pl.when(cap >= d)
        def _():
            s = cap - d
            audio_part(s)

            @pl.when(cap == ncap - 1)
            def _():
                first_send(s, left_slot(s, d), -1)
        return carry

    lax.fori_loop(0, ncap - 1, audio_parts, 0)
    audio_part(cap)

    def relay_one(s, h, slot, step):
        landed(s, h)
        asend[s, h] = (akeep[s, h] + arecv[s, h].astype(jnp.float32)).astype(jnp.bfloat16)
        line_sum_copy(s, h, slot, step).start()

    def relay(d):
        for h in range(2):
            @pl.when(jnp.logical_and(cap >= 1, cap + d < ncap))
            def _():
                relay_one(cap + d, h, cap + d, 1)

            @pl.when(jnp.logical_and(cap + 1 < ncap, cap >= d))
            def _():
                s = cap - d
                relay_one(s, h, left_slot(s, d), -1)

    groups = nclip // 2
    chip, parity = clip // 2, clip % 2
    audio_student = abuf.at[1].reshape(rows, width)

    def pair_copy(q):
        return remote(psend.at[q], precv.at[q], ps_send.at[q], ps_recv.at[q], flip(clip, 1), cap)

    def text_copy(q, offset):
        return remote(tsend.at[q], trecv.at[offset], ts_send.at[offset], ts_recv.at[offset], q * 2 + parity, cap)

    def text_step(i, carry):
        @pl.when(i < groups)
        def _():
            q = (chip + 1 + i) % groups
            cs = pl.ds(pl.multiple_of(q * (2 * shard), LANE), 2 * shard)
            grad = 10.0 * lax.dot_general(
                rmat[:, cs], audio_student[...], (((0,), (0,)), ((), ())),
                preferred_element_type=jnp.float32)
            for g in range(2):
                @pl.when(parity == g)
                def _():
                    psend[q] = grad[(1 - g) * shard:(2 - g) * shard, :].astype(jnp.bfloat16)
                    tkeep[q] = grad[g * shard:(g + 1) * shard, :]
            pair_copy(q).start()

        @pl.when(i >= 1)
        def _():
            q = (chip + i) % groups
            pair_copy(q).wait_recv()
            both = tkeep[q] + precv[q].astype(jnp.float32)

            @pl.when(i < groups)
            def _():
                tsend[q] = both.astype(jnp.bfloat16)
                text_copy(q, i).start()

            @pl.when(i == groups)
            def _():
                tg_ref[...] = both
        return carry

    middle = max(groups // 2, 1)
    lax.fori_loop(0, middle, text_step, 0)

    def relays(i, carry):
        relay(ncap - 2 - i)
        return carry

    lax.fori_loop(0, ncap - 3, relays, 0)
    lax.fori_loop(middle, groups + 1, text_step, 0)
    if ncap > 2:
        relay(1)

    for t in range(2):
        for mask in range(1, nclip):
            bit = mask & -mask
            for cand in orders[t]:
                if mask & cand:
                    bit = cand
            tree_copy(t, mask ^ bit, bit).wait_send()

        def drain(s, carry, t=t):
            @pl.when(jnp.logical_and(s <= cap, cap + 1 < ncap))
            def _():
                for h in range(2):
                    line_copy(t, s, h, 1, False).wait_send()

            @pl.when(jnp.logical_and(s >= cap, cap >= 1))
            def _():
                for h in range(2):
                    line_copy(t, s, h, -1, False).wait_send()
            return carry
        lax.fori_loop(0, ncap, drain, 0)

    def drain_sums(s, carry):
        @pl.when(s != cap)
        def _():
            for h in range(2):
                line_sum_copy(s, h, s, 0).wait_send()
        return carry
    lax.fori_loop(0, ncap, drain_sums, 0)

    def drain_pairs(q, carry):
        pair_copy(q).wait_send()
        return carry
    lax.fori_loop(0, groups, drain_pairs, 0)

    total = tg_ref[...]
    for j in range(1, groups):
        copy = text_copy(chip, j)
        copy.wait_recv()
        copy.wait_send()
        total = total + trecv[j].astype(jnp.float32)
    tg_ref[...] = total

    for h in range(2):
        ag_ref[h * half_rows:(h + 1) * half_rows, :] = akeep[cap, h]

        def add(slot, h=h):
            landed(slot, h)
            ag_ref[h * half_rows:(h + 1) * half_rows, :] += arecv[slot, h].astype(jnp.float32)

        @pl.when(cap >= 1)
        def _():
            add(cap)

        @pl.when(cap + 1 < ncap)
        def _():
            add(ncap)


def body(nclip, ncap, teacher_audio, teacher_text, student_audio, student_text):
    shard, width = teacher_audio.shape
    rows, cols = shard * ncap, shard * nclip
    f32, bf16 = jnp.float32, jnp.bfloat16
    roomy = rows * cols <= 2 ** 21
    dma = pltpu.SemaphoreType.DMA
    return pl.pallas_call(
        functools.partial(kernel, nclip, ncap, shard),
        out_shape=(jax.ShapeDtypeStruct((shard, width), f32),) * 2,
        in_specs=[pl.BlockSpec(memory_space=pltpu.VMEM)] * 4,
        out_specs=(pl.BlockSpec(memory_space=pltpu.VMEM),) * 2,
        scratch_shapes=[
            pltpu.VMEM((2, ncap, shard, width), bf16),
            pltpu.VMEM((2, nclip, shard, width), bf16),
            pltpu.VMEM((rows, cols), f32),
            pltpu.VMEM((rows, cols) if roomy else (8, LANE), f32),
            pltpu.VMEM((rows, cols), bf16),
            pltpu.VMEM((shard, cols), f32),
            pltpu.VMEM((rows, LANE), f32),
            pltpu.VMEM((rows, LANE), f32),
            pltpu.VMEM((rows, LANE), f32),
            pltpu.VMEM((8, cols), f32),
            pltpu.VMEM((rows, LANE), f32),
            pltpu.VMEM((rows, LANE), f32),
            pltpu.VMEM((rows, LANE), f32),
            pltpu.VMEM((ITERS, ncap, 1, rows), f32),
            pltpu.VMEM((ITERS, nclip, 1, cols), f32),
            pltpu.VMEM((ncap, 1, rows), f32),
            pltpu.VMEM((ncap, 3, rows), f32),
            pltpu.VMEM((ncap, 2, shard // 2, width), f32),
            pltpu.VMEM((ncap, 2, shard // 2, width), bf16),
            pltpu.VMEM((ncap + 1, 2, shard // 2, width), bf16),
            pltpu.VMEM((nclip // 2, shard, width), f32),
            pltpu.VMEM((nclip // 2, shard, width), bf16),
            pltpu.VMEM((nclip // 2, shard, width), bf16),
            pltpu.VMEM((nclip // 2, shard, width), bf16),
            pltpu.VMEM((nclip // 2, shard, width), bf16),
            dma((2, 2, ncap, 2)), dma((2, ncap, 2)),
            dma((2, nclip)), dma((2, nclip)),
            dma((ITERS + 1, ncap)), dma((ITERS + 1, ncap)),
            dma((ITERS, nclip)), dma((ITERS, nclip)),
            dma((ncap, 2)), dma((ncap + 1, 2)),
            dma((nclip // 2,)), dma((nclip // 2,)),
            dma((nclip // 2,)), dma((nclip // 2,)),
        ],
        compiler_params=pltpu.CompilerParams(
            collective_id=0, has_side_effects=True, vmem_limit_bytes=66 * 1000 * 1000),
    )(teacher_audio, teacher_text, student_audio, student_text)


def solution(mesh):
    nclip, ncap = mesh.shape["clip"], mesh.shape["cap"]
    placed = (
        P(("clip", "cap"), None),
        P(("cap", "clip"), None),
        P(("clip", "cap"), None),
        P(("cap", "clip"), None),
    )
    return jax.shard_map(
        functools.partial(body, nclip, ncap),
        mesh=mesh,
        in_specs=placed,
        out_specs=(P(("clip", "cap"), None), P(("cap", "clip"), None)),
        check_vma=False,
    )
```

```python
import functools

import jax
import jax.numpy as jnp
from jax import lax
from jax.experimental import pallas as pl
from jax.experimental.pallas import tpu as pltpu
from jax.sharding import PartitionSpec as P

ITERS = 3
LANE = 128
MESH = pl.DeviceIdType.MESH


def flip(index, bit):
    return index + bit * (1 - 2 * ((index // bit) % 2))


def flip_mask(index, mask, count):
    bit = 1
    while bit < count:
        if mask & bit:
            index = flip(index, bit)
        bit *= 2
    return index


def tree_orders(count):
    bits = []
    bit = 2
    while bit < count:
        bits.append(bit)
        bit *= 2
    tail = [1] if count > 1 else []
    return (bits + tail, bits[::-1] + tail)


def children(mask, order):
    last = -1
    for position, bit in enumerate(order):
        if mask & bit:
            last = position
    return [bit for bit in order[last + 1:]]


def mask_sequence(count, order):
    out, level = [], [0]
    while level:
        following = []
        for mask in level:
            for bit in children(mask, order):
                following.append(mask | bit)
        out.extend(following)
        level = following
    return out


def kernel(
    nclip, ncap, shard,
    ta_ref, tt_ref, sa_ref, st_ref, out_ref,
    abuf, tbuf, kmat, smat, rmat, lbuf, pbuf, wrep, srep, crep, mrep, smax, ssum,
    rowx, colx, maxx, lastx, akeep, asend, arecv, tkeep, psend, precv, tsend, trecv,
    az_send, az_recv, tx_send, tx_recv, rx_send, rx_recv, cx_send, cx_recv,
    as_send, as_recv, ps_send, ps_recv, ts_send, ts_recv,
):
    clip = lax.axis_index("clip")
    cap = lax.axis_index("cap")
    rows, cols, width = shard * ncap, shard * nclip, ta_ref.shape[1]
    tiles = cols // LANE
    ag_ref, tg_ref = out_ref.at[0], out_ref.at[1]
    orders = tree_orders(nclip)
    if smat.shape != kmat.shape:
        smat = rmat

    def remote(src, dst, ss, rs, to_clip, to_cap):
        return pltpu.make_async_remote_copy(
            src_ref=src, dst_ref=dst, send_sem=ss, recv_sem=rs,
            device_id=(to_clip, to_cap), device_id_type=MESH)

    barrier = pltpu.get_barrier_semaphore()
    for j in range(1, ncap):
        pl.semaphore_signal(barrier, inc=1, device_id=(clip, lax.rem(cap + j, ncap)), device_id_type=MESH)
    for j in range(1, nclip):
        pl.semaphore_signal(barrier, inc=1, device_id=(lax.rem(clip + j, nclip), cap), device_id_type=MESH)

    for t, (a, x) in enumerate(((ta_ref, tt_ref), (sa_ref, st_ref))):
        abuf[t, cap] = a[...]
        tbuf[t, clip] = x[...]
    pl.semaphore_wait(barrier, ncap + nclip - 2)

    own_audio, own_text = (ta_ref, sa_ref), (tt_ref, st_ref)

    def tree_copy(t, mask, bit):
        src_index = flip_mask(clip, mask, nclip)
        src = own_text[t] if mask == 0 else tbuf.at[t, src_index]
        return remote(src, tbuf.at[t, src_index], tx_send.at[t, mask | bit],
                      tx_recv.at[t, mask | bit], flip(clip, bit), cap)

    def tree_forward(t, mask):
        for bit in children(mask, orders[t]):
            tree_copy(t, mask, bit).start()

    def tree_wait(t, mask):
        landed = tbuf.at[t, flip_mask(clip, mask, nclip)]
        remote(landed, landed, tx_send.at[t, mask], tx_recv.at[t, mask], clip, cap).wait_recv()

    def line_copy(t, s, h, step, own):
        part = pl.ds(h * (shard // 2), shard // 2)
        dst = abuf.at[t, s, part, :]
        src = own_audio[t].at[part, :] if own else dst
        side = 0 if step < 0 else 1
        return remote(src, dst, az_send.at[t, side, s, h], az_recv.at[t, s, h], clip, cap + step)

    def line_own(t):
        for h in range(2):
            @pl.when(cap + 1 < ncap)
            def _():
                line_copy(t, cap, h, 1, True).start()

            @pl.when(cap >= 1)
            def _():
                line_copy(t, cap, h, -1, True).start()

    def line_left(t, d, h):
        s = cap - d
        line_copy(t, s, h, 1, False).wait_recv()

        @pl.when(cap + 1 < ncap)
        def _():
            line_copy(t, s, h, 1, False).start()

    def line_right(t, d, h):
        s = cap + d
        line_copy(t, s, h, -1, False).wait_recv()

        @pl.when(cap >= 1)
        def _():
            line_copy(t, s, h, -1, False).start()

    def line_step(t, d):
        for h in range(2):
            @pl.when(cap >= d)
            def _():
                line_left(t, d, h)

            @pl.when(cap + d < ncap)
            def _():
                line_right(t, d, h)

    step_cols = 512 if cols % 512 == 0 else LANE

    def logits(t, s):
        rs = pl.ds(pl.multiple_of(s * shard, shard), shard)
        a = abuf[t, s]
        text = tbuf.at[t].reshape(cols, width)
        top = None
        for j in range(0, cols, step_cols):
            part = 10.0 * lax.dot_general(
                a, text[j:j + step_cols, :], (((1,), (1,)), ((), ())),
                preferred_element_type=jnp.float32)
            lbuf[:, j:j + step_cols] = part
            here = jnp.max(part, axis=1, keepdims=True)
            top = here if top is None else jnp.maximum(top, here)
        total = None
        for j in range(0, cols, step_cols):
            value = jnp.exp(lbuf[:, j:j + step_cols] - top)
            if t == 0:
                kmat[rs, j:j + step_cols] = value
            else:
                smat[rs, j:j + step_cols] = value.astype(smat.dtype)
                here = jnp.sum(value, axis=1, keepdims=True)
                total = here if total is None else total + here
        wide = jnp.broadcast_to(top, (shard, LANE))
        if t == 0:
            mrep[rs, :] = wide
        else:
            smax[rs, :] = wide
            ssum[rs, :] = jnp.broadcast_to(total, (shard, LANE))

    tree_forward(0, 0)
    line_own(0)
    sequence = mask_sequence(nclip, orders[0])
    waited = len(orders[0])
    if ncap > 2:
        line_step(0, 1)
    for mask in sequence[:waited]:
        tree_wait(0, mask)
        tree_forward(0, mask)
    for d in range(2, ncap - 1):
        line_step(0, d)
    for mask in sequence[waited:]:
        tree_wait(0, mask)
        tree_forward(0, mask)
    tree_forward(1, 0)
    line_own(1)
    logits(0, cap)

    def early(t, d):
        @pl.when(cap >= d)
        def _():
            logits(t, cap - d)

        @pl.when(cap + d < ncap)
        def _():
            logits(t, cap + d)

    def early_loop(t, first, last):
        def one(d, carry):
            early(t, d)
            return carry
        lax.fori_loop(first, last, one, 0)

    if ncap > 1:
        def one_teacher(d, carry):
            @pl.when(d == ncap - 1)
            def _():
                if ncap > 2:
                    line_step(0, ncap - 1)
                else:
                    line_step(0, 1)
            early(0, d)
            return carry
        lax.fori_loop(1, ncap, one_teacher, 0)

    def spread(buffer, sends, recvs, k, along_cap):
        count, me = (ncap, cap) if along_cap else (nclip, clip)
        for j in range(1, count):
            peer = lax.rem(me + j, count)
            remote(buffer.at[0], buffer.at[j], sends.at[k, j], recvs.at[k, j],
                   clip if along_cap else peer, peer if along_cap else cap).start()

    def gathered(buffer, sends, recvs, k, along_cap):
        count = ncap if along_cap else nclip
        for j in range(1, count):
            copy = remote(buffer.at[0], buffer.at[j], sends.at[k, j], recvs.at[k, j], clip, cap)
            copy.wait_recv()

    def across(ref):
        return ref[...].T[0:1, :]

    def down(vector):
        return jnp.broadcast_to(vector, (LANE, rows)).T

    block = 64

    def column_pass():
        def one(i, carry):
            rs = pl.ds(pl.multiple_of(i * block, block), block)
            w = wrep[rs, :]
            out = []
            for t in range(tiles):
                product = kmat[rs, t * LANE:(t + 1) * LANE] * w
                out.append(carry[t] + jnp.sum(product.reshape(block // 8, 8, LANE), axis=0))
            return tuple(out)
        acc = lax.fori_loop(0, rows // block, one, tuple(jnp.zeros((8, LANE), jnp.float32) for _ in range(tiles)))
        return [jnp.sum(a, axis=0, keepdims=True) for a in acc]

    def row_pass():
        def one(i, carry):
            rs = pl.ds(pl.multiple_of(i * block, block), block)
            acc = jnp.zeros((block // 8, 8, LANE), jnp.float32)
            for t in range(tiles):
                acc = acc + kmat[rs, t * LANE:(t + 1) * LANE].reshape(block // 8, 8, LANE) * crep[:, t * LANE:(t + 1) * LANE][None]
            pbuf[rs, :] = acc.reshape(block, LANE)
            return carry
        lax.fori_loop(0, rows // block, one, 0)
        return jnp.sum(pbuf[...].T, axis=0, keepdims=True)

    student_sequence = mask_sequence(nclip, orders[1])
    half = nclip // 2

    def student_trees(masks):
        for mask in masks:
            tree_wait(1, mask)
            tree_forward(1, mask)

    def fill_max():
        student_trees(student_sequence[:half])
        if ncap > 1:
            line_step(1, 1)

    def fill_column_0():
        student_trees(student_sequence[half:])
        for d in range(2, ncap - 1):
            line_step(1, d)

    def fill_row_0():
        if ncap > 2:
            line_step(1, ncap - 1)
        logits(1, cap)

    cuts = [1, 1 + (ncap - 1) // 3, 1 + 2 * (ncap - 1) // 3, ncap]

    fills = {
        ("c", 0): fill_column_0,
        ("r", 0): fill_row_0,
        ("c", 1): lambda: early_loop(1, cuts[0], cuts[1]),
        ("r", 1): lambda: early_loop(1, cuts[1], cuts[2]),
        ("c", 2): lambda: early_loop(1, cuts[2], cuts[3]),
    }

    local_max = across(mrep)
    maxx[0] = local_max
    spread(maxx, rx_send, rx_recv, 0, True)
    fill_max()
    gathered(maxx, rx_send, rx_recv, 0, True)
    top = maxx[0]
    for j in range(1, ncap):
        top = jnp.maximum(top, maxx[j])
    factor = jnp.exp(maxx[0] - top)
    wrep[...] = down(factor)

    for it in range(ITERS):
        for t, part in enumerate(column_pass()):
            colx[it, 0, :, t * LANE:(t + 1) * LANE] = part
        spread(colx.at[it], cx_send, cx_recv, it, False)
        fills[("c", it)]()
        gathered(colx.at[it], cx_send, cx_recv, it, False)
        column = colx[it, 0]
        for j in range(1, nclip):
            column = column + colx[it, j]
        crep[...] = jnp.broadcast_to(1.0 / column, (8, cols))
        row = row_pass() * factor
        if it < ITERS - 1:
            rowx[it, 0] = row
            spread(rowx.at[it], rx_send, rx_recv, it + 1, True)
            fills[("r", it)]()
            gathered(rowx.at[it], rx_send, rx_recv, it + 1, True)
            total = rowx[it, 0]
            for j in range(1, ncap):
                total = total + rowx[it, j]
        else:
            lastx[0, 0:1, :] = row
            lastx[0, 1:2, :] = across(smax)
            lastx[0, 2:3, :] = across(ssum)
            spread(lastx, rx_send, rx_recv, it + 1, True)
            gathered(lastx, rx_send, rx_recv, it + 1, True)
            total = lastx[0, 0:1, :]
            best = lastx[0, 1:2, :]
            for j in range(1, ncap):
                total = total + lastx[j, 0:1, :]
                best = jnp.maximum(best, lastx[j, 1:2, :])
            own = jnp.exp(lastx[0, 1:2, :] - best)
            norm = own * lastx[0, 2:3, :]
            for j in range(1, ncap):
                norm = norm + jnp.exp(lastx[j, 1:2, :] - best) * lastx[j, 2:3, :]
            srep[...] = down(own / norm)
        wrep[...] = down(factor / total)

    text_student = tbuf.at[1].reshape(cols, width)
    half_rows = shard // 2

    def line_sum_copy(s, h, slot, step):
        return remote(asend.at[s, h], arecv.at[slot, h], as_send.at[s, h], as_recv.at[slot, h], clip, cap + step)

    def landed(slot, h):
        here = arecv.at[slot, h]
        remote(here, here, as_send.at[0, h], as_recv.at[slot, h], clip, cap).wait_recv()

    def audio_part(s):
        rs = pl.ds(pl.multiple_of(s * shard, shard), shard)
        w, p = wrep[rs, :], srep[rs, :]
        for t in range(tiles):
            cs = slice(t * LANE, (t + 1) * LANE)
            target = (w * kmat[rs, cs]) * crep[0:1, cs]
            rmat[rs, cs] = (smat[rs, cs].astype(jnp.float32) * p - target).astype(jnp.bfloat16)
        grad = jnp.dot(rmat[rs, :], text_student[...], preferred_element_type=jnp.float32)
        for h in range(2):
            akeep[s, h] = grad[h * half_rows:(h + 1) * half_rows, :]

    def first_send(s, slot, step):
        for h in range(2):
            asend[s, h] = akeep[s, h].astype(jnp.bfloat16)
            line_sum_copy(s, h, slot, step).start()

    def left_slot(s, d):
        return s + (ncap - s) * (1 // d)

    def audio_parts(i, carry):
        d = ncap - 1 - i

        @pl.when(cap + d < ncap)
        def _():
            s = cap + d
            audio_part(s)

            @pl.when(cap == 0)
            def _():
                first_send(s, s, 1)

        @pl.when(cap >= d)
        def _():
            s = cap - d
            audio_part(s)

            @pl.when(cap == ncap - 1)
            def _():
                first_send(s, left_slot(s, d), -1)
        return carry

    lax.fori_loop(0, ncap - 1, audio_parts, 0)
    audio_part(cap)

    def relay_one(s, h, slot, step):
        landed(s, h)
        asend[s, h] = (akeep[s, h] + arecv[s, h].astype(jnp.float32)).astype(jnp.bfloat16)
        line_sum_copy(s, h, slot, step).start()

    def relay(d):
        for h in range(2):
            @pl.when(jnp.logical_and(cap >= 1, cap + d < ncap))
            def _():
                relay_one(cap + d, h, cap + d, 1)

            @pl.when(jnp.logical_and(cap + 1 < ncap, cap >= d))
            def _():
                s = cap - d
                relay_one(s, h, left_slot(s, d), -1)

    groups = nclip // 2
    chip, parity = clip // 2, clip % 2
    audio_student = abuf.at[1].reshape(rows, width)

    def pair_copy(q):
        return remote(psend.at[q], precv.at[q], ps_send.at[q], ps_recv.at[q], flip(clip, 1), cap)

    def text_copy(q, offset):
        return remote(tsend.at[q], trecv.at[offset], ts_send.at[offset], ts_recv.at[offset], q * 2 + parity, cap)

    def text_step(i, carry):
        @pl.when(i < groups)
        def _():
            q = (chip + 1 + i) % groups
            cs = pl.ds(pl.multiple_of(q * (2 * shard), LANE), 2 * shard)
            grad = lax.dot_general(
                rmat[:, cs], audio_student[...], (((0,), (0,)), ((), ())),
                preferred_element_type=jnp.float32)
            for g in range(2):
                @pl.when(parity == g)
                def _():
                    psend[q] = grad[(1 - g) * shard:(2 - g) * shard, :].astype(jnp.bfloat16)
                    tkeep[q] = grad[g * shard:(g + 1) * shard, :]
            pair_copy(q).start()

        @pl.when(i >= 1)
        def _():
            q = (chip + i) % groups
            pair_copy(q).wait_recv()
            both = tkeep[q] + precv[q].astype(jnp.float32)

            @pl.when(i < groups)
            def _():
                tsend[q] = both.astype(jnp.bfloat16)
                text_copy(q, i).start()

            @pl.when(i == groups)
            def _():
                tg_ref[...] = both
        return carry

    middle = max(groups // 2, 1)
    lax.fori_loop(0, middle, text_step, 0)

    def relays(i, carry):
        relay(ncap - 2 - i)
        return carry

    lax.fori_loop(0, ncap - 3, relays, 0)
    lax.fori_loop(middle, groups + 1, text_step, 0)
    if ncap > 2:
        relay(1)

    for k in range(ITERS + 1):
        buffer = maxx if k == 0 else lastx if k == ITERS else rowx.at[k - 1]
        for j in range(1, ncap):
            remote(buffer.at[0], buffer.at[j], rx_send.at[k, j], rx_recv.at[k, j], clip, cap).wait_send()
    for k in range(ITERS):
        for j in range(1, nclip):
            remote(colx.at[k, 0], colx.at[k, j], cx_send.at[k, j], cx_recv.at[k, j], clip, cap).wait_send()
    for t in range(2):
        for mask in range(1, nclip):
            bit = mask & -mask
            for cand in orders[t]:
                if mask & cand:
                    bit = cand
            tree_copy(t, mask ^ bit, bit).wait_send()

        def drain(s, carry, t=t):
            @pl.when(jnp.logical_and(s <= cap, cap + 1 < ncap))
            def _():
                for h in range(2):
                    line_copy(t, s, h, 1, False).wait_send()

            @pl.when(jnp.logical_and(s >= cap, cap >= 1))
            def _():
                for h in range(2):
                    line_copy(t, s, h, -1, False).wait_send()
            return carry
        lax.fori_loop(0, ncap, drain, 0)

    def drain_sums(s, carry):
        @pl.when(s != cap)
        def _():
            for h in range(2):
                line_sum_copy(s, h, s, 0).wait_send()
        return carry
    lax.fori_loop(0, ncap, drain_sums, 0)

    def drain_pairs(q, carry):
        pair_copy(q).wait_send()
        return carry
    lax.fori_loop(0, groups, drain_pairs, 0)

    total = tg_ref[...]
    for j in range(1, groups):
        copy = text_copy(chip, j)
        copy.wait_recv()
        copy.wait_send()
        total = total + trecv[j].astype(jnp.float32)
    tg_ref[...] = total

    for h in range(2):
        ag_ref[h * half_rows:(h + 1) * half_rows, :] = akeep[cap, h]

        def add(slot, h=h):
            landed(slot, h)
            ag_ref[h * half_rows:(h + 1) * half_rows, :] += arecv[slot, h].astype(jnp.float32)

        @pl.when(cap >= 1)
        def _():
            add(cap)

        @pl.when(cap + 1 < ncap)
        def _():
            add(ncap)


def body(nclip, ncap, teacher_audio, teacher_text, student_audio, student_text):
    shard, width = teacher_audio.shape
    rows, cols = shard * ncap, shard * nclip
    f32, bf16 = jnp.float32, jnp.bfloat16
    roomy = rows * cols <= 2 ** 21
    dma = pltpu.SemaphoreType.DMA
    grads = pl.pallas_call(
        functools.partial(kernel, nclip, ncap, shard),
        out_shape=jax.ShapeDtypeStruct((2, shard, width), f32),
        in_specs=[pl.BlockSpec(memory_space=pltpu.VMEM)] * 4,
        out_specs=pl.BlockSpec(memory_space=pltpu.VMEM),
        scratch_shapes=[
            pltpu.VMEM((2, ncap, shard, width), bf16),
            pltpu.VMEM((2, nclip, shard, width), bf16),
            pltpu.VMEM((rows, cols), f32),
            pltpu.VMEM((rows, cols) if roomy else (8, LANE), f32),
            pltpu.VMEM((rows, cols), bf16),
            pltpu.VMEM((shard, cols), f32),
            pltpu.VMEM((rows, LANE), f32),
            pltpu.VMEM((rows, LANE), f32),
            pltpu.VMEM((rows, LANE), f32),
            pltpu.VMEM((8, cols), f32),
            pltpu.VMEM((rows, LANE), f32),
            pltpu.VMEM((rows, LANE), f32),
            pltpu.VMEM((rows, LANE), f32),
            pltpu.VMEM((ITERS, ncap, 1, rows), f32),
            pltpu.VMEM((ITERS, nclip, 1, cols), f32),
            pltpu.VMEM((ncap, 1, rows), f32),
            pltpu.VMEM((ncap, 3, rows), f32),
            pltpu.VMEM((ncap, 2, shard // 2, width), f32),
            pltpu.VMEM((ncap, 2, shard // 2, width), bf16),
            pltpu.VMEM((ncap + 1, 2, shard // 2, width), bf16),
            pltpu.VMEM((nclip // 2, shard, width), f32),
            pltpu.VMEM((nclip // 2, shard, width), bf16),
            pltpu.VMEM((nclip // 2, shard, width), bf16),
            pltpu.VMEM((nclip // 2, shard, width), bf16),
            pltpu.VMEM((nclip // 2, shard, width), bf16),
            dma((2, 2, ncap, 2)), dma((2, ncap, 2)),
            dma((2, nclip)), dma((2, nclip)),
            dma((ITERS + 1, ncap)), dma((ITERS + 1, ncap)),
            dma((ITERS, nclip)), dma((ITERS, nclip)),
            dma((ncap, 2)), dma((ncap + 1, 2)),
            dma((nclip // 2,)), dma((nclip // 2,)),
            dma((nclip // 2,)), dma((nclip // 2,)),
        ],
        compiler_params=pltpu.CompilerParams(
            collective_id=0, has_side_effects=True, vmem_limit_bytes=66 * 1000 * 1000),
    )(teacher_audio, teacher_text, student_audio, student_text)
    return 10.0 * grads[0], 10.0 * grads[1]


def solution(mesh):
    nclip, ncap = mesh.shape["clip"], mesh.shape["cap"]
    placed = (
        P(("clip", "cap"), None),
        P(("cap", "clip"), None),
        P(("clip", "cap"), None),
        P(("cap", "clip"), None),
    )
    return jax.shard_map(
        functools.partial(body, nclip, ncap),
        mesh=mesh,
        in_specs=placed,
        out_specs=(P(("clip", "cap"), None), P(("cap", "clip"), None)),
        check_vma=False,
    )
```
